32 devices in a mesh: ctx: 8 (over z, x), tp: 4 (over y, core).
Axes of the slice: x: 2, y: 2, z: 4, core: 2. Of those that a mesh axis runs over, the one named last changes fastest.
Arguments:
- hidden_input: bfloat16 [256, 8192], P(None, 'ctx'), may hold values from -6 to 6
- w_query: bfloat16 [8192, 8192], P('ctx', 'tp')
- key_value_weight: bfloat16 [8192, 2, 1024], P('ctx', None, 'tp'), may hold values from -0.0625 to 0.0625
- w_out: bfloat16 [8192, 8192], P('tp', 'ctx'), may hold values from -0.0625 to 0.0625
- key_value_cache: bfloat16 [2, 8, 32768, 128], P(None, 'tp', 'ctx'), may hold values from -6 to 6
- filled: int32 [8], P('ctx'), may hold values from 512 to 4096, as said below
- positions: int32 [256], replicated, may hold values from 0 to 255, each once
Outputs:
- layer_out: bfloat16 [256, 8192], P('tp', 'ctx')
The draws below stay inside these ranges and needn't reach their ends.
Inputs may be any that keep to these rules, and one draw needn't show every extreme that they name: `filled`: every shard has at least 512 used slots; some shard is full and some holds exactly 512.
All inputs are finite; a program needn't handle non-finite values.
Results may differ from the reference program's by a relative error of at most 0.0045.
The reference program's roundings to bfloat16 on the way count: a program that leaves them out, or rounds other values in their place, can miss the bound.
Values may be sent and summed in bfloat16 or wider, within the bound.
A program may use at most 128 MiB of HBM per device.

```python
import math
import jax
import jax.numpy as jnp
from jax import lax

MODEL_WIDTH = 8192
HQ = 64
KEY_HEADS = 8
HEAD_SIZE = 128
QUERY_GROUP = 8
NEW_TOKENS = 256
S_DEV = 4096
SHARDS = 8
CACHE_SLOTS = 32768


def draw_filled(key, part):
    amounts = jax.random.randint(jax.random.fold_in(key, 11), (SHARDS,), S_DEV // 8, S_DEV + 1, dtype=jnp.int32)
    shuffled = jax.random.permutation(jax.random.fold_in(key, 12), SHARDS)
    amounts = amounts.at[shuffled[0]].set(S_DEV)
    amounts = amounts.at[shuffled[1]].set(S_DEV // 8)
    return amounts.astype(jnp.int32)


def draw_w_query(key, part):
    entry_key = jax.random.fold_in(key, 21)
    entries = jnp.clip(jax.random.normal(entry_key, (MODEL_WIDTH, HQ, HEAD_SIZE), jnp.float32), -6.0, 6.0)
    strengths = jnp.array([20.0, 40.0, 70.0], jnp.float32)
    chosen = jax.random.permutation(jax.random.fold_in(key, 22), HQ)[:3]
    head_scales = jnp.ones((HQ,), jnp.float32).at[chosen].set(strengths)
    scaled = entries * head_scales[None, :, None] * (1.0 / math.sqrt(MODEL_WIDTH))
    return scaled.reshape(MODEL_WIDTH, HQ * HEAD_SIZE).astype(jnp.bfloat16)


def levels(key, dims, cuts, low, top_value):
    def one(position, parts):
        heights = jax.random.uniform(jax.random.fold_in(jax.random.fold_in(key, 6), position), (parts,), jnp.float32, low / len(cuts), top_value / len(cuts))
        return jnp.repeat(jnp.exp(heights), dims[position] // parts).reshape((-1,) + (1,) * (len(dims) - position - 1))

    level = one(*cuts[0])
    for cut in cuts[1:]:
        level = level * one(*cut)
    return level


def gaussian(rng, dims, deviation, limit, cuts=(), held_as=jnp.bfloat16):
    values = deviation * jax.random.normal(rng, dims, jnp.float32)
    if cuts:
        values = values * levels(rng, dims, cuts, -0.22, 0.18)
    return jnp.clip(values, -limit, limit).astype(held_as)


def setup_inputs(seed: int = 0) -> dict:
    keys = jax.random.split(jax.random.key(seed), 8)
    return {
        "hidden_input": gaussian(keys[0], (NEW_TOKENS, MODEL_WIDTH), 1.0, 6.0, ((1, 8),)),
        "w_query": draw_w_query(jax.random.fold_in(keys[7], 71), 0),
        "key_value_weight": gaussian(keys[2], (MODEL_WIDTH, 2, KEY_HEADS * HEAD_SIZE), MODEL_WIDTH ** -0.5, 0.0625, ((0, 8), (2, 4))),
        "w_out": gaussian(keys[3], (HQ * HEAD_SIZE, MODEL_WIDTH), (HQ * HEAD_SIZE) ** -0.5, 0.0625, ((0, 4), (1, 8))),
        "key_value_cache": gaussian(keys[4], (2, KEY_HEADS, CACHE_SLOTS, HEAD_SIZE), 1.0, 6.0, ((1, 4), (2, 8))),
        "filled": draw_filled(jax.random.fold_in(keys[7], 71), 0),
        "positions": jax.random.permutation(keys[6], NEW_TOKENS).astype(jnp.int32),
    }


NEG_FILL = -1e+30

def attend(query_rows, key_rows, val_rows, visible):
    scores = jnp.einsum('grd,sd->grs', query_rows.astype(jnp.float32), key_rows.astype(jnp.float32)) / math.sqrt(HEAD_SIZE)
    scores = jnp.where(visible, scores, NEG_FILL)
    row_max = lax.optimization_barrier(jnp.max(scores, axis=-1))
    probs = jnp.exp(scores - row_max[..., None])
    denom = lax.optimization_barrier(jnp.sum(probs, axis=-1))
    probs_low = probs.astype(jnp.bfloat16)
    output = jnp.einsum('grs,sd->grd', probs_low.astype(jnp.float32), val_rows.astype(jnp.float32)) / denom[..., None]
    return (row_max + jnp.log(denom), output)

def reference(hidden_input, w_query, key_value_weight, w_out, key_value_cache, filled, positions):
    query_rows = jnp.dot(hidden_input, w_query, preferred_element_type=jnp.float32).astype(jnp.bfloat16)
    query_rows = query_rows.reshape(NEW_TOKENS, KEY_HEADS, QUERY_GROUP, HEAD_SIZE)
    key_value_rows = jnp.dot(hidden_input, key_value_weight.reshape(MODEL_WIDTH, 2 * KEY_HEADS * HEAD_SIZE), preferred_element_type=jnp.float32).astype(jnp.bfloat16)
    key_value_rows = key_value_rows.reshape(NEW_TOKENS, 2, KEY_HEADS, HEAD_SIZE)
    causal_mask = positions[None, :] <= positions[:, None]

    def head_results(group):
        head_queries = jnp.transpose(query_rows[:, group], (1, 0, 2))
        key_all = key_value_cache[0][group]
        val_all = key_value_cache[1][group]

        def per_shard(shard):
            begin = (shard * S_DEV).astype(jnp.int32)
            key_rows = lax.dynamic_slice_in_dim(key_all, begin, S_DEV, 0)
            val_rows = lax.dynamic_slice_in_dim(val_all, begin, S_DEV, 0)
            visible = jnp.arange(S_DEV, dtype=jnp.int32) < filled[shard]
            return attend(head_queries, key_rows, val_rows, visible[None, None, :])
        log_sums, outputs = lax.map(per_shard, jnp.arange(SHARDS, dtype=jnp.int32))
        new_log, new_out = attend(head_queries, key_value_rows[:, 0, group], key_value_rows[:, 1, group], causal_mask[None])
        all_log = jnp.concatenate([log_sums, new_log[None]], axis=0)
        all_out = jnp.concatenate([outputs, new_out[None]], axis=0)
        top_log = lax.optimization_barrier(jnp.max(all_log, axis=0))
        shares = jnp.exp(all_log - top_log[None])
        merged = lax.optimization_barrier(jnp.sum(shares[..., None] * all_out, axis=0)) / lax.optimization_barrier(jnp.sum(shares, axis=0))[..., None]
        return merged.astype(jnp.bfloat16)
    head_output = lax.map(head_results, jnp.arange(KEY_HEADS, dtype=jnp.int32))
    attended = jnp.transpose(head_output, (2, 0, 1, 3)).reshape(NEW_TOKENS, HQ * HEAD_SIZE)
    return jnp.dot(attended, w_out, preferred_element_type=jnp.float32).astype(jnp.bfloat16)
```

```python
import functools
import math

import jax
import jax.numpy as jnp
from jax import lax
from jax.experimental import pallas as pl
from jax.experimental.pallas import tpu as pltpu
from jax.sharding import PartitionSpec as P

MESH = pl.DeviceIdType.MESH
HIDE = -1e30
LOG2E = 1.4426950408889634


def factor(shards):
    for inner in (8, 2) if shards > 8 else (2,):
        if shards % inner == 0:
            return shards // inner, inner
    return shards, 1


def greet(peers):
    barrier = pltpu.get_barrier_semaphore()
    for peer in peers:
        pl.semaphore_signal(barrier, inc=1, device_id=peer, device_id_type=MESH)
    pl.semaphore_wait(barrier, len(peers))


def peers_of(outer, inner):
    me = lax.axis_index("ctx")
    z = me // inner
    x = me % inner
    xs = [(x + d) % inner for d in range(1, inner)]
    zs = [(z + d) % outer for d in range(1, outer)]
    x_ids = [{"ctx": z * inner + v} for v in xs]
    z_ids = [{"ctx": v * inner + x} for v in zs]
    return x, z, xs, zs, x_ids, z_ids


def remote(src, dst, sems, place, peer):
    return pltpu.make_async_remote_copy(
        src_ref=src,
        dst_ref=dst,
        send_sem=sems[0].at[place],
        recv_sem=sems[1].at[place],
        device_id=peer,
        device_id_type=MESH,
    )


def project_kernel(
    outer, inner, q_blocks,
    hid_ref, wq_ref, wkv_ref,
    q_ref, kv_ref,
    w_buf, part_x, recv_x, acc, recv_z,
    w_sem, sx, rx, sz, rz, gz, hz, gx, hx,
):
    blocks = q_blocks + 1
    rows = acc.shape[2]
    cols = acc.shape[3]
    x, z, xs, zs, x_ids, z_ids = peers_of(outer, inner)
    loads = []
    for b in range(blocks):
        src = wq_ref.at[:, pl.ds(b * cols, cols)] if b < q_blocks else wkv_ref
        load = pltpu.make_async_copy(src, w_buf.at[b], w_sem.at[b])
        load.start()
        loads.append(load)
    greet(x_ids + z_ids)
    def ship(b):
        loads[b].wait()
        copies = []
        for d, peer in enumerate(x_ids):
            part_x[b, d] = jnp.dot(
                hid_ref[xs[d]], w_buf[b], preferred_element_type=jnp.float32
            )
            copy = remote(part_x.at[b, d], recv_x.at[b, d], (sx, rx), (b, d), peer)
            copy.start()
            copies.append(copy)
        own = jnp.dot(hid_ref[x], w_buf[b], preferred_element_type=jnp.float32)
        acc[b] = own.reshape(outer, rows, cols)
        return copies

    def add_x(b, x_copies):
        copies = []
        for copy in x_copies:
            copy.wait_recv()
        total = acc[b]
        for d in range(inner - 1):
            total += recv_x[b, d].reshape(outer, rows, cols)
        acc[b] = total
        for d, peer in enumerate(z_ids):
            copy = remote(acc.at[b, zs[d]], recv_z.at[b, d], (sz, rz), (b, d), peer)
            copy.start()
            copies.append(copy)
        return copies

    def add_z(b, z_copies):
        for copy in z_copies:
            copy.wait_recv()
        total = acc[b, z]
        for d in range(outer - 1):
            total += recv_z[b, d]
        low = total.astype(jnp.bfloat16)
        copies = []
        if b == q_blocks:
            kv_ref[...] = low
            return copies
        q_ref[b, x, z] = low
        for d, peer in enumerate(z_ids):
            copy = remote(q_ref.at[b, x, z], q_ref.at[b, x, z], (gz, hz), (b, d), peer)
            copy.start()
            copies.append(copy)
        return copies

    def spread(b, z_copies):
        copies = []
        for copy in z_copies:
            copy.wait_recv()
        for d, peer in enumerate(x_ids):
            copy = remote(q_ref.at[b, x], q_ref.at[b, x], (gx, hx), (b, d), peer)
            copy.start()
            copies.append(copy)
        return copies

    first = [ship(b) for b in range(blocks)]
    second, third, fourth = {}, {}, {}
    for t in range(blocks + 2):
        if t < blocks:
            second[t] = add_x(t, first[t])
        if 0 <= t - 1 < blocks:
            third[t - 1] = add_z(t - 1, second[t - 1])
        if 0 <= t - 2 < q_blocks:
            fourth[t - 2] = spread(t - 2, third[t - 2])
    for b in range(q_blocks):
        for copy in fourth[b]:
            copy.wait_recv()
    for group in (first, list(second.values()), list(third.values()), list(fourth.values())):
        for copies in group:
            for copy in copies:
                copy.wait_send()


def project(hidden, w_query, w_kv, outer, inner):
    tokens, width = hidden.shape
    shards = outer * inner
    rows = tokens // shards
    cols = w_kv.shape[1]
    q_blocks = w_query.shape[1] // cols
    blocks = q_blocks + 1
    dma = pltpu.SemaphoreType.DMA
    vmem = pl.BlockSpec(memory_space=pltpu.VMEM)
    hbm = pl.BlockSpec(memory_space=pl.ANY)
    nx, nz = max(inner - 1, 1), max(outer - 1, 1)
    return pl.pallas_call(
        functools.partial(project_kernel, outer, inner, q_blocks),
        out_shape=(
            jax.ShapeDtypeStruct((q_blocks, inner, outer, rows, cols), jnp.bfloat16),
            jax.ShapeDtypeStruct((rows, cols), jnp.bfloat16),
        ),
        in_specs=[vmem, hbm, hbm],
        out_specs=(vmem, vmem),
        scratch_shapes=[
            pltpu.VMEM((blocks, width, cols), jnp.bfloat16),
            pltpu.VMEM((blocks, nx, outer * rows, cols), jnp.float32),
            pltpu.VMEM((blocks, nx, outer * rows, cols), jnp.float32),
            pltpu.VMEM((blocks, outer, rows, cols), jnp.float32),
            pltpu.VMEM((blocks, nz, rows, cols), jnp.float32),
            dma((blocks,)),
            dma((blocks, nx)), dma((blocks, nx)),
            dma((blocks, nz)), dma((blocks, nz)),
            dma((q_blocks, nz)), dma((q_blocks, nz)),
            dma((q_blocks, nx)), dma((q_blocks, nx)),
        ],
        compiler_params=pltpu.CompilerParams(
            collective_id=0, has_side_effects=True, vmem_limit_bytes=48 << 20
        ),
        name="project",
    )(hidden.reshape(inner, outer * rows, width), w_query, w_kv)


def attend_kernel(
    scale, kb,
    filled_ref, q_ref, k_ref, v_ref, kn_ref, vn_ref, posq_ref, posk_ref,
    o_ref, lse_ref,
    k_aug, v_aug, score,
):
    g, h = pl.program_id(0), pl.program_id(1)
    slots = k_ref.shape[2]
    tokens, dim = q_ref.shape[1], q_ref.shape[2]
    extra = posk_ref.shape[1]
    filled = filled_ref[0]
    lane = lax.broadcasted_iota(jnp.int32, (1, dim), 1)

    @pl.when((g == 0) & (h == 0))
    def _():
        lse_ref[...] = jnp.zeros_like(lse_ref)

    @pl.when(h == 0)
    def _():
        k_aug[:, :dim] = k_ref[0, 0]
        v_aug[:slots, :dim] = v_ref[0, 0]
        row = lax.broadcasted_iota(jnp.int32, (slots, dim), 0)
        col = lax.broadcasted_iota(jnp.int32, (slots, dim), 1)
        k_aug[:, dim:] = jnp.where(
            (row >= filled) & (col == 0), HIDE, 0.0
        ).astype(jnp.bfloat16)
        v_aug[slots:, :] = jnp.zeros((extra, 2 * dim), jnp.bfloat16)
        v_aug[slots : slots + kn_ref.shape[0], :dim] = vn_ref[...]
        v_aug[:, dim:] = jnp.where(
            lax.broadcasted_iota(jnp.int32, (slots + extra, dim), 1) == 0, 1.0, 0.0
        ).astype(jnp.bfloat16)

    q = q_ref[0]
    q_aug = jnp.concatenate(
        [q, jnp.broadcast_to(jnp.where(lane == 0, 1.0, 0.0).astype(jnp.bfloat16), q.shape)], axis=1
    )
    nt = (((1,), (1,)), ((), ()))
    kn = jnp.concatenate(
        [kn_ref[...], jnp.zeros((extra - kn_ref.shape[0], dim), jnp.bfloat16)], axis=0
    ) if extra > kn_ref.shape[0] else kn_ref[...]
    fresh = lax.dot_general(q, kn, nt, preferred_element_type=jnp.float32)
    fresh = jnp.where(posk_ref[...] <= posq_ref[...], fresh, HIDE)
    score[:, slots:] = fresh
    top = fresh
    for b in range(slots // kb):
        part = lax.dot_general(
            q_aug, k_aug[b * kb : (b + 1) * kb, :], nt, preferred_element_type=jnp.float32
        )
        score[:, b * kb : (b + 1) * kb] = part
        for j in range(kb // dim):
            top = jnp.maximum(top, part[:, j * dim : (j + 1) * dim])
    peak = jnp.max(top, axis=1, keepdims=True)
    shift = peak * (scale * LOG2E)
    total = None
    for b in range(slots // kb + 1):
        lo = b * kb
        hi = min(lo + kb, slots + extra)
        probs = jnp.exp2(score[:, lo:hi] * (scale * LOG2E) - shift).astype(jnp.bfloat16)
        term = jnp.dot(probs, v_aug[lo:hi, :], preferred_element_type=jnp.float32)
        total = term if total is None else total + term
    denom = total[:, dim : dim + 1]
    o_ref[0] = (total[:, :dim] / denom).astype(o_ref.dtype)
    head = g * pl.num_programs(1) + h
    lse_ref[...] = jnp.where(lane == head, peak * scale + jnp.log(denom), lse_ref[...])


def attend(q, kv_new, cache, filled, positions, own_positions, scale):
    q_blocks, tokens, cols = q.shape
    _, kv_heads, slots, dim = cache.shape
    per = cols // dim
    group = q_blocks * per // kv_heads
    rows = kv_new.shape[0]
    extra = 128
    padded = jnp.concatenate(
        [own_positions, jnp.full((extra - rows,), tokens + 1, jnp.int32)]
    )
    once = pl.BlockSpec((tokens, 1), lambda g, h: (0, 0))
    return pl.pallas_call(
        functools.partial(attend_kernel, scale, math.gcd(slots, 512)),
        grid=(kv_heads, group),
        out_shape=(
            jax.ShapeDtypeStruct((q_blocks, tokens, cols), jnp.bfloat16),
            jax.ShapeDtypeStruct((tokens, 128), jnp.float32),
        ),
        in_specs=[
            pl.BlockSpec(memory_space=pltpu.SMEM),
            pl.BlockSpec(
                (1, tokens, dim), lambda g, h: ((g * group + h) // per, 0, (g * group + h) % per)
            ),
            pl.BlockSpec((1, 1, slots, dim), lambda g, h: (0, g, 0, 0)),
            pl.BlockSpec((1, 1, slots, dim), lambda g, h: (1, g, 0, 0)),
            pl.BlockSpec((rows, dim), lambda g, h: (0, g)),
            pl.BlockSpec((rows, dim), lambda g, h: (0, kv_heads + g)),
            once,
            pl.BlockSpec((1, extra), lambda g, h: (0, 0)),
        ],
        out_specs=(
            pl.BlockSpec(
                (1, tokens, dim), lambda g, h: ((g * group + h) // per, 0, (g * group + h) % per)
            ),
            pl.BlockSpec((tokens, 128), lambda g, h: (0, 0)),
        ),
        scratch_shapes=[
            pltpu.VMEM((slots, 2 * dim), jnp.bfloat16),
            pltpu.VMEM((slots + extra, 2 * dim), jnp.bfloat16),
            pltpu.VMEM((tokens, slots + extra), jnp.float32),
        ],
        compiler_params=pltpu.CompilerParams(
            dimension_semantics=("arbitrary", "arbitrary"), vmem_limit_bytes=40 << 20
        ),
        name="attend",
    )(
        filled, q, cache, cache, kv_new, kv_new,
        positions.reshape(tokens, 1), padded.reshape(1, extra),
    )


def merge_kernel(
    outer, inner, tp_size, dim,
    o_ref, lse_ref, w_ref,
    out_ref,
    w_buf, att, recv_x, lse_x, mid, mid_lse, recv_z, lse_z, part, part_low, recv_t,
    w_sem, slx, rlx, sx, rx, slz, rlz, sz, rz, gz, hz, gx, hx, st, rt,
):
    blocks = o_ref.shape[0]
    rows = att.shape[3]
    cols = att.shape[4]
    per = cols // dim
    x, z, xs, zs, x_ids, z_ids = peers_of(outer, inner)
    tp = lax.axis_index("tp")
    ts = [(tp + d) % tp_size for d in range(1, tp_size)]
    t_ids = [{"tp": v} for v in ts]
    load = pltpu.make_async_copy(w_ref, w_buf, w_sem)
    load.start()
    greet(x_ids + z_ids + t_ids)
    sent = []

    def go(*args):
        copy = remote(*args)
        copy.start()
        sent.append(copy)
        return copy

    def shares(logs):
        top = functools.reduce(jnp.maximum, logs)
        weights = [jnp.exp(v - top) for v in logs]
        total = sum(weights[1:], weights[0])
        return [w / total for w in weights], top + jnp.log(total)

    def blend(b, weights, values):
        pieces = []
        for j in range(per):
            head = b * per + j
            acc = None
            for w, v in zip(weights, values):
                term = w[:, head : head + 1] * v[:, j * dim : (j + 1) * dim].astype(jnp.float32)
                acc = term if acc is None else acc + term
            pieces.append(acc)
        return jnp.concatenate(pieces, axis=1).astype(jnp.bfloat16)

    lx = [
        go(lse_ref.at[xs[d]], lse_x.at[d], (slx, rlx), d, peer) for d, peer in enumerate(x_ids)
    ]
    ox = [
        [go(o_ref.at[b, xs[d]], recv_x.at[b, d], (sx, rx), (b, d), peer) for d, peer in enumerate(x_ids)]
        for b in range(blocks)
    ]
    for copy in lx:
        copy.wait_recv()
    x_weights, x_log = shares([lse_ref[x]] + [lse_x[d] for d in range(inner - 1)])
    mid_lse[...] = x_log.reshape(outer, rows, 128)
    lz = [
        go(mid_lse.at[zs[d]], lse_z.at[d], (slz, rlz), d, peer) for d, peer in enumerate(z_ids)
    ]
    oz, az, ax = {}, {}, {}
    z_weights = None
    for t in range(blocks + 2):
        if t < blocks:
            b = t
            for copy in ox[b]:
                copy.wait_recv()
            merged = blend(b, x_weights, [o_ref[b, x]] + [recv_x[b, d] for d in range(inner - 1)])
            mid[b] = merged.reshape(outer, rows, cols)
            oz[b] = [
                go(mid.at[b, zs[d]], recv_z.at[b, d], (sz, rz), (b, d), peer)
                for d, peer in enumerate(z_ids)
            ]
        if 0 <= t - 1 < blocks:
            b = t - 1
            if z_weights is None:
                for copy in lz:
                    copy.wait_recv()
                z_weights, _ = shares([mid_lse[z]] + [lse_z[d] for d in range(outer - 1)])
            for copy in oz[b]:
                copy.wait_recv()
            att[b, x, z] = blend(
                b, z_weights, [mid[b, z]] + [recv_z[b, d] for d in range(outer - 1)]
            )
            az[b] = [
                go(att.at[b, x, z], att.at[b, x, z], (gz, hz), (b, d), peer)
                for d, peer in enumerate(z_ids)
            ]
        if 0 <= t - 2 < blocks:
            b = t - 2
            for copy in az[b]:
                copy.wait_recv()
            ax[b] = [
                go(att.at[b, x], att.at[b, x], (gx, hx), (b, d), peer)
                for d, peer in enumerate(x_ids)
            ]
    load.wait()
    half = outer * rows
    for d, v in enumerate([x] + xs):
        for b in range(blocks):
            if d > 0:
                ax[b][inner - 1 - d].wait_recv()
            term = jnp.dot(
                att[b, v].reshape(half, cols),
                w_buf[b * cols : (b + 1) * cols, :],
                preferred_element_type=jnp.float32,
            )
            if b == 0:
                part[v] = term
            else:
                part[v] += term
    share = out_ref.shape[0]
    whole = part[...].reshape(tp_size, share, part.shape[2])
    part_low[...] = whole.astype(jnp.bfloat16)
    rt_copies = [
        go(part_low.at[ts[d]], recv_t.at[d], (st, rt), d, peer) for d, peer in enumerate(t_ids)
    ]
    own = part.reshape(tp_size, share, part.shape[2])[tp]
    for d, copy in enumerate(rt_copies):
        copy.wait_recv()
        own += recv_t[d].astype(jnp.float32)
    out_ref[...] = own.astype(out_ref.dtype)
    for copy in sent:
        copy.wait_send()


def merge(o, lse, w_out, outer, inner, dim):
    blocks, tokens, cols = o.shape
    rows = tokens // (outer * inner)
    half = outer * rows
    tp_size = lax.axis_size("tp")
    width = w_out.shape[1]
    share = tokens // tp_size
    nx, nz, nt = max(inner - 1, 1), max(outer - 1, 1), max(tp_size - 1, 1)
    dma = pltpu.SemaphoreType.DMA
    vmem = pl.BlockSpec(memory_space=pltpu.VMEM)
    low, full = jnp.bfloat16, jnp.float32
    return pl.pallas_call(
        functools.partial(merge_kernel, outer, inner, tp_size, dim),
        out_shape=jax.ShapeDtypeStruct((share, width), low),
        in_specs=[vmem, vmem, pl.BlockSpec(memory_space=pl.ANY)],
        out_specs=vmem,
        scratch_shapes=[
            pltpu.VMEM(w_out.shape, low),
            pltpu.VMEM((blocks, inner, outer, rows, cols), low),
            pltpu.VMEM((blocks, nx, half, cols), low),
            pltpu.VMEM((nx, half, 128), full),
            pltpu.VMEM((blocks, outer, rows, cols), low),
            pltpu.VMEM((outer, rows, 128), full),
            pltpu.VMEM((blocks, nz, rows, cols), low),
            pltpu.VMEM((nz, rows, 128), full),
            pltpu.VMEM((inner, half, width), full),
            pltpu.VMEM((tp_size, share, width), low),
            pltpu.VMEM((nt, share, width), low),
            dma(()),
            dma((nx,)), dma((nx,)),
            dma((blocks, nx)), dma((blocks, nx)),
            dma((nz,)), dma((nz,)),
            dma((blocks, nz)), dma((blocks, nz)),
            dma((blocks, nz)), dma((blocks, nz)),
            dma((blocks, nx)), dma((blocks, nx)),
            dma((nt,)), dma((nt,)),
        ],
        compiler_params=pltpu.CompilerParams(
            collective_id=1, has_side_effects=True, vmem_limit_bytes=48 << 20
        ),
        name="merge",
    )(o.reshape(blocks, inner, half, cols), lse.reshape(inner, half, 128), w_out)


def body(hidden_input, w_query, key_value_weight, w_out, key_value_cache, filled, positions):
    tokens, width = hidden_input.shape
    shards = lax.axis_size("ctx")
    outer, inner = factor(shards)
    rows = tokens // shards
    dim = key_value_cache.shape[3]
    q, kv_new = project(
        hidden_input, w_query, key_value_weight.reshape(width, -1), outer, inner
    )
    me = lax.axis_index("ctx")
    chunk = (me % inner) * outer + me // inner
    own_positions = lax.dynamic_slice_in_dim(positions, chunk * rows, rows, 0)
    o, lse = attend(
        q.reshape(q.shape[0], tokens, q.shape[-1]),
        kv_new, key_value_cache, filled, positions, own_positions, 1.0 / math.sqrt(dim),
    )
    return merge(o, lse, w_out, outer, inner, dim)


def solution(mesh):
    placed = (
        P(None, "ctx"),
        P("ctx", "tp"),
        P("ctx", None, "tp"),
        P("tp", "ctx"),
        P(None, "tp", "ctx", None),
        P("ctx"),
        P(),
    )
    return jax.shard_map(
        body, mesh=mesh, in_specs=placed, out_specs=P("tp", "ctx"), check_vma=False
    )
```

```python
import functools
import math

import jax
import jax.numpy as jnp
from jax import lax
from jax.experimental import pallas as pl
from jax.experimental.pallas import tpu as pltpu
from jax.sharding import PartitionSpec as P

MESH = pl.DeviceIdType.MESH
HIDE = -1e30
LOG2E = 1.4426950408889634


def factor(shards):
    for inner in (8, 2) if shards > 8 else (2,):
        if shards % inner == 0:
            return shards // inner, inner
    return shards, 1


def greet(peers):
    barrier = pltpu.get_barrier_semaphore()
    for peer in peers:
        pl.semaphore_signal(barrier, inc=1, device_id=peer, device_id_type=MESH)
    pl.semaphore_wait(barrier, len(peers))


def peers_of(outer, inner):
    me = lax.axis_index("ctx")
    z = me // inner
    x = me % inner
    xs = [(x + d) % inner for d in range(1, inner)]
    zs = [(z + d) % outer for d in range(1, outer)]
    x_ids = [{"ctx": z * inner + v} for v in xs]
    z_ids = [{"ctx": v * inner + x} for v in zs]
    return x, z, xs, zs, x_ids, z_ids


def remote(src, dst, sems, place, peer):
    return pltpu.make_async_remote_copy(
        src_ref=src,
        dst_ref=dst,
        send_sem=sems[0].at[place],
        recv_sem=sems[1].at[place],
        device_id=peer,
        device_id_type=MESH,
    )


NT = (((1,), (1,)), ((), ()))


def layer_kernel(
    outer, inner, tp_size, kv_heads, dim, scale, kb,
    filled_ref, hid_ref, posq_ref, posk_ref, wq_ref, wkv_ref, cache_ref, wo_ref,
    out_ref,
    w_buf, k_aug, v_raw, v_aug, wo_buf,
    part_x, recv_x, acc, recv_z, kv_new, q_buf,
    o_buf, lse, o_recv, lse_recv, mid, mid_lse, mid_recv, mid_lse_recv, weights, att,
    part, part_low, recv_t,
    w_sem, k_sem, v_sem, wo_sem,
    s1, r1, s2, r2, s3, r3, s4, r4, s5, r5, s6, r6, s7, r7, s8, r8, s9, r9, sa, ra, st, rt,
):
    cw = kv_heads * dim
    per = kv_heads
    q_blocks = q_buf.shape[0]
    blocks = q_blocks + 2
    group = q_blocks * per // kv_heads
    rows = acc.shape[2]
    half = outer * rows
    tokens = inner * half
    slots = v_raw.shape[1]
    chunk = cw // outer
    x, z, xs, zs, x_ids, z_ids = peers_of(outer, inner)
    tp = lax.axis_index("tp")
    ts = [(tp + d) % tp_size for d in range(1, tp_size)]
    t_ids = [{"tp": v} for v in ts]

    loads = [
        pltpu.make_async_copy(wkv_ref, w_buf.at[:, pl.ds(0, 2 * cw)], w_sem.at[0]),
        pltpu.make_async_copy(wq_ref, w_buf.at[:, pl.ds(2 * cw, q_blocks * cw)], w_sem.at[1]),
    ]
    k_loads = [
        pltpu.make_async_copy(cache_ref.at[0, g], k_aug.at[g, :, pl.ds(0, dim)], k_sem.at[g])
        for g in range(kv_heads)
    ]
    v_loads = [
        pltpu.make_async_copy(cache_ref.at[1, g], v_raw.at[g], v_sem.at[g])
        for g in range(kv_heads)
    ]
    wo_load = pltpu.make_async_copy(wo_ref, wo_buf, wo_sem)
    for load in loads + k_loads + v_loads + [wo_load]:
        load.start()
    greet(x_ids + z_ids + t_ids)
    for load in loads:
        load.wait()

    def x1(b):
        return [remote(part_x.at[b, d], recv_x.at[b, d], (s1, r1), (b, d), p)
                for d, p in enumerate(x_ids)]

    def z1(b):
        return [remote(acc.at[b, zs[d]], recv_z.at[b, d], (s2, r2), (b, d), p)
                for d, p in enumerate(z_ids)]

    def zg(i):
        return [remote(q_buf.at[i, x, z], q_buf.at[i, x, z], (s3, r3), (i, d), p)
                for d, p in enumerate(z_ids)]

    def xg(i):
        return [remote(q_buf.at[i, x], q_buf.at[i, x], (s4, r4), (i, d), p)
                for d, p in enumerate(x_ids)]

    def xl(i):
        return [remote(lse.at[i, xs[d]], lse_recv.at[i, d], (s5, r5), (i, d), p)
                for d, p in enumerate(x_ids)]

    def xo(i):
        return [remote(o_buf.at[i, xs[d]], o_recv.at[i, d], (s6, r6), (i, d), p)
                for d, p in enumerate(x_ids)]

    def zl(i):
        return [remote(mid_lse.at[i], mid_lse_recv.at[i, d], (s7, r7), (i, d), p)
                for d, p in enumerate(z_ids)]

    def zo(i):
        return [remote(mid.at[i, zs[d]], mid_recv.at[i, d], (s8, r8), (i, d), p)
                for d, p in enumerate(z_ids)]

    def za(i):
        return [remote(att.at[x, i, z], att.at[x, i, z], (s9, r9), (i, d), p)
                for d, p in enumerate(z_ids)]

    def xa(i):
        return [remote(att.at[x, i], att.at[x, i], (sa, ra), (i, d), p)
                for d, p in enumerate(x_ids)]

    def start(copies):
        for copy in copies:
            copy.start()

    def arrive(copies):
        for copy in copies:
            copy.wait_recv()

    def ship(b):
        w = w_buf[:, pl.ds(pl.multiple_of(b * cw, cw), cw)]
        for d in range(inner - 1):
            part_x[b, d] = jnp.dot(hid_ref[xs[d]], w, preferred_element_type=jnp.float32)
        start(x1(b))
        own = jnp.dot(hid_ref[x], w, preferred_element_type=jnp.float32)
        acc[b] = own.reshape(outer, rows, cw)

    def add_x(b):
        arrive(x1(b))
        total = acc[b]
        for d in range(inner - 1):
            total += recv_x[b, d].reshape(outer, rows, cw)
        acc[b] = total
        start(z1(b))

    def add_z(b):
        arrive(z1(b))
        total = acc[b, z]
        for d in range(outer - 1):
            total += recv_z[b, d]
        low = total.astype(jnp.bfloat16)

        @pl.when(b < 2)
        def _():
            kv_new[b] = low

        @pl.when(b >= 2)
        def _():
            q_buf[b - 2, x, z] = low
            start(zg(b - 2))

    def spread(i):
        arrive(zg(i))
        start(xg(i))

    def attend(i):
        arrive(xg(i))
        g = i * per // group
        c = scale * LOG2E
        lane = lax.broadcasted_iota(jnp.int32, (tokens, dim), 1)
        one = jnp.where(lane == 0, 1.0, 0.0).astype(jnp.bfloat16)
        q = q_buf[i].reshape(tokens, cw)
        qs = [q[:, j * dim : (j + 1) * dim] for j in range(per)]
        aug = [jnp.concatenate([v, one], axis=1) for v in qs]
        k_fresh = kv_new[0, :, pl.ds(pl.multiple_of(g * dim, dim), dim)]
        v_fresh = kv_new[1, :, pl.ds(pl.multiple_of(g * dim, dim), dim)]
        v_fresh = v_fresh.astype(jnp.float32).T
        v_fresh = jnp.concatenate(
            [v_fresh, jnp.ones((16, rows), jnp.float32)], axis=0
        ).astype(jnp.bfloat16)
        seen = posk_ref[...] <= posq_ref[...]

        def scores(j, b):
            if b < 0:
                return jnp.where(seen, lax.dot_general(
                    k_fresh, qs[j], NT, preferred_element_type=jnp.float32), HIDE)
            return lax.dot_general(
                k_aug[g, b * kb : (b + 1) * kb, :], aug[j], NT, preferred_element_type=jnp.float32
            )

        order = [(j, b) for b in list(range(slots // kb)) + [-1] for j in range(per)]
        state = [None] * per
        coming = scores(*order[0])
        for n, (j, b) in enumerate(order):
            s = coming
            if n + 1 < len(order):
                coming = scores(*order[n + 1])
            high = jnp.max(s, axis=0, keepdims=True)
            if state[j] is not None:
                high = jnp.maximum(state[j][0], high)
            p = jnp.exp2((s - high) * c).astype(jnp.bfloat16)
            v = v_fresh if b < 0 else v_aug[g, :, b * kb : (b + 1) * kb]
            t = jnp.dot(v, p, preferred_element_type=jnp.float32)
            if state[j] is not None:
                t = t + state[j][1] * jnp.exp2((state[j][0] - high) * c)
            state[j] = (high, t)
        for j in range(per):
            high, t = state[j]
            denom = t[dim : dim + 1, :]
            value = (t[:dim] / denom).astype(jnp.bfloat16)
            log = high * scale + jnp.log(denom)
            for v in range(inner):
                o_buf[i, v, j * dim : (j + 1) * dim, :] = value[:, v * half : (v + 1) * half]
                lse[i, v, j : j + 1, :] = log[:, v * half : (v + 1) * half]
        start(xl(i))
        start(xo(i))

    def shares(logs):
        top = functools.reduce(jnp.maximum, logs)
        parts = [jnp.exp(v - top) for v in logs]
        total = sum(parts[1:], parts[0])
        return [w / total for w in parts], top + jnp.log(total)

    def blend_x(i):
        arrive(xl(i))
        ws, log = shares([lse[i, x]] + [lse_recv[i, d] for d in range(inner - 1)])
        mid_lse[i] = log
        start(zl(i))
        arrive(xo(i))
        pieces = []
        for j in range(per):
            span = slice(j * dim, (j + 1) * dim)
            total = ws[0][j : j + 1] * o_buf[i, x, span, :].astype(jnp.float32)
            for d in range(inner - 1):
                total += ws[d + 1][j : j + 1] * o_recv[i, d, span, :].astype(jnp.float32)
            pieces.append(total.reshape(dim // chunk, chunk, half).astype(jnp.bfloat16))
        for j in range(per):
            n = dim // chunk
            mid[i, j * n : (j + 1) * n] = pieces[j]
        start(zo(i))

    def blend_z(i):
        arrive(zl(i))
        ws, _ = shares([mid_lse[i]] + [mid_lse_recv[i, d] for d in range(outer - 1)])
        for d in range(outer):
            weights[d] = ws[d]
        head = z * chunk // dim
        arrive(zo(i))
        total = weights[0, pl.ds(head, 1), :] * mid[i, z].astype(jnp.float32)
        for d in range(outer - 1):
            total += weights[d + 1, pl.ds(head, 1), :] * mid_recv[i, d].astype(jnp.float32)
        att[x, i, z] = total.astype(jnp.bfloat16)
        start(za(i))

    def spread_att(i):
        arrive(za(i))
        start(xa(i))

    ahead = 2
    for b in range(ahead):
        ship(b)
    lse[...] = jnp.zeros_like(lse)
    filled = filled_ref[0]
    row = lax.broadcasted_iota(jnp.int32, (slots, dim), 0)
    col = lax.broadcasted_iota(jnp.int32, (slots, dim), 1)
    bias = jnp.where((row >= filled) & (col == 0), HIDE, 0.0).astype(jnp.bfloat16)
    for g in range(kv_heads):
        k_aug[g, :, dim:] = bias
        v_aug[g, dim:, :] = jnp.ones((16, slots), jnp.bfloat16)
        v_loads[g].wait()
        v_aug[g, :dim, :] = v_raw[g].T
        k_loads[g].wait()

    def step(t, carry):
        def stage(lag, first, last, run):
            i = t - lag

            @pl.when((i >= first) & (i < last))
            def _():
                run(i)

        stage(-ahead, ahead, blocks, ship)
        stage(0, 0, blocks, add_x)
        stage(1, 0, blocks, add_z)
        stage(4, 0, q_blocks, spread)
        stage(5, 0, q_blocks, attend)
        stage(6, 0, q_blocks, blend_x)
        stage(7, 0, q_blocks, blend_z)
        stage(8, 0, q_blocks, spread_att)
        return carry

    lax.fori_loop(0, q_blocks + 8, step, 0)

    wo_load.wait()
    for d, v in enumerate([x] + xs):
        if d > 0:
            for i in range(q_blocks):
                xa(i)[inner - 1 - d].wait_recv()
        lhs = att[v].reshape(q_blocks * cw, half).T
        part[v] = jnp.dot(lhs, wo_buf[...], preferred_element_type=jnp.float32)
    share = out_ref.shape[0]
    whole = part[...].reshape(tp_size, share, part.shape[2])
    part_low[...] = whole.astype(jnp.bfloat16)
    last = [remote(part_low.at[ts[d]], recv_t.at[d], (st, rt), d, p) for d, p in enumerate(t_ids)]
    start(last)
    own = part.reshape(tp_size, share, part.shape[2])[tp]
    for d, copy in enumerate(last):
        copy.wait_recv()
        own += recv_t[d].astype(jnp.float32)
    out_ref[...] = own.astype(out_ref.dtype)
    for copy in last:
        copy.wait_send()

    def drain(kinds):
        def run(i, carry):
            for kind in kinds:
                for copy in kind(i):
                    copy.wait_send()
            return carry
        return run

    lax.fori_loop(0, blocks, drain([x1, z1]), 0)
    lax.fori_loop(0, q_blocks, drain([zg, xg, xl, xo, zl, zo, za, xa]), 0)


def body(hidden_input, w_query, key_value_weight, w_out, key_value_cache, filled, positions):
    tokens, width = hidden_input.shape
    shards = lax.axis_size("ctx")
    tp_size = lax.axis_size("tp")
    outer, inner = factor(shards)
    rows = tokens // shards
    half = outer * rows
    _, kv_heads, slots, dim = key_value_cache.shape
    cw = kv_heads * dim
    q_blocks = w_query.shape[1] // cw
    blocks = q_blocks + 2
    chunk = cw // outer
    out_width = w_out.shape[1]
    share = tokens // tp_size
    me = lax.axis_index("ctx")
    owned = (me % inner) * outer + me // inner
    own_positions = lax.dynamic_slice_in_dim(positions, owned * rows, rows, 0)
    nx, nz, nt = max(inner - 1, 1), max(outer - 1, 1), max(tp_size - 1, 1)
    dma = pltpu.SemaphoreType.DMA
    vmem = pl.BlockSpec(memory_space=pltpu.VMEM)
    hbm = pl.BlockSpec(memory_space=pl.ANY)
    low, full = jnp.bfloat16, jnp.float32
    pairs = []
    for count, peers in (
        (blocks, nx), (blocks, nz), (q_blocks, nz), (q_blocks, nx), (q_blocks, nx),
        (q_blocks, nx), (q_blocks, nz), (q_blocks, nz), (q_blocks, nz), (q_blocks, nx),
    ):
        pairs += [dma((count, peers)), dma((count, peers))]
    return pl.pallas_call(
        functools.partial(
            layer_kernel, outer, inner, tp_size, kv_heads, dim, 1.0 / math.sqrt(dim),
            math.gcd(slots, 1024),
        ),
        out_shape=jax.ShapeDtypeStruct((share, out_width), low),
        in_specs=[pl.BlockSpec(memory_space=pltpu.SMEM), vmem, vmem, vmem, hbm, hbm, hbm, hbm],
        out_specs=vmem,
        scratch_shapes=[
            pltpu.VMEM((width, blocks * cw), low),
            pltpu.VMEM((kv_heads, slots, 2 * dim), low),
            pltpu.VMEM((kv_heads, slots, dim), low),
            pltpu.VMEM((kv_heads, dim + 16, slots), low),
            pltpu.VMEM(w_out.shape, low),
            pltpu.VMEM((blocks, nx, half, cw), full),
            pltpu.VMEM((blocks, nx, half, cw), full),
            pltpu.VMEM((blocks, outer, rows, cw), full),
            pltpu.VMEM((blocks, nz, rows, cw), full),
            pltpu.VMEM((2, rows, cw), low),
            pltpu.VMEM((q_blocks, inner, outer, rows, cw), low),
            pltpu.VMEM((q_blocks, inner, cw, half), low),
            pltpu.VMEM((q_blocks, inner, 8, half), full),
            pltpu.VMEM((q_blocks, nx, cw, half), low),
            pltpu.VMEM((q_blocks, nx, 8, half), full),
            pltpu.VMEM((q_blocks, outer, chunk, half), low),
            pltpu.VMEM((q_blocks, 8, half), full),
            pltpu.VMEM((q_blocks, nz, chunk, half), low),
            pltpu.VMEM((q_blocks, nz, 8, half), full),
            pltpu.VMEM((outer, 8, half), full),
            pltpu.VMEM((inner, q_blocks, outer, chunk, half), low),
            pltpu.VMEM((inner, half, out_width), full),
            pltpu.VMEM((tp_size, share, out_width), low),
            pltpu.VMEM((nt, share, out_width), low),
            dma((2,)), dma((kv_heads,)), dma((kv_heads,)), dma(()),
            *pairs,
            dma((nt,)), dma((nt,)),
        ],
        compiler_params=pltpu.CompilerParams(
            collective_id=0, has_side_effects=True, vmem_limit_bytes=60 << 20
        ),
        name="layer",
    )(
        filled, hidden_input.reshape(inner, half, width), positions.reshape(1, tokens),
        own_positions.reshape(rows, 1), w_query, key_value_weight.reshape(width, -1),
        key_value_cache, w_out,
    )


def solution(mesh):
    placed = (
        P(None, "ctx"),
        P("ctx", "tp"),
        P("ctx", None, "tp"),
        P("tp", "ctx"),
        P(None, "tp", "ctx", None),
        P("ctx"),
        P(),
    )
    return jax.shard_map(
        body, mesh=mesh, in_specs=placed, out_specs=P("tp", "ctx"), check_vma=False
    )
```

```python
import functools
import math

import jax
import jax.numpy as jnp
from jax import lax
from jax.experimental import pallas as pl
from jax.experimental.pallas import tpu as pltpu
from jax.sharding import PartitionSpec as P

MESH = pl.DeviceIdType.MESH
HIDE = -1e30
LOG2E = 1.4426950408889634


def factor(shards):
    for inner in (8, 2) if shards > 8 else (2,):
        if shards % inner == 0:
            return shards // inner, inner
    return shards, 1


def greet(peers):
    barrier = pltpu.get_barrier_semaphore()
    for peer in peers:
        pl.semaphore_signal(barrier, inc=1, device_id=peer, device_id_type=MESH)
    pl.semaphore_wait(barrier, len(peers))


def peers_of(outer, inner):
    me = lax.axis_index("ctx")
    z = me // inner
    x = me % inner
    xs = [(x + d) % inner for d in range(1, inner)]
    zs = [(z + d) % outer for d in range(1, outer)]
    x_ids = [{"ctx": z * inner + v} for v in xs]
    z_ids = [{"ctx": v * inner + x} for v in zs]
    return x, z, xs, zs, x_ids, z_ids


def remote(src, dst, sems, place, peer):
    return pltpu.make_async_remote_copy(
        src_ref=src,
        dst_ref=dst,
        send_sem=sems[0].at[place],
        recv_sem=sems[1].at[place],
        device_id=peer,
        device_id_type=MESH,
    )


NT = (((1,), (1,)), ((), ()))


def layer_kernel(
    outer, inner, tp_size, kv_heads, dim, scale, kb,
    filled_ref, hid_ref, posq_ref, wq_ref, wkv_ref, cache_ref, wo_ref,
    out_ref,
    w_buf, k_aug, v_raw, v_aug, wo_buf,
    part_x, recv_x, acc, recv_z, kv_new, q_buf,
    o_buf, lse, o_recv, lse_recv, mid, mid_lse, mid_recv, mid_lse_recv, weights, att,
    part, part_low, recv_t, places,
    w_sem, k_sem, v_sem, wo_sem,
    s1, r1, s2, r2, s3, r3, s4, r4, s5, r5, s6, r6, s7, r7, s8, r8, s9, r9, sa, ra, st, rt,
):
    cw = kv_heads * dim
    per = kv_heads
    q_blocks = q_buf.shape[0]
    blocks = q_blocks + 2
    group = q_blocks * per // kv_heads
    rows = acc.shape[2]
    half = outer * rows
    tokens = inner * half
    slots = v_raw.shape[1]
    chunk = cw // outer
    x, z, xs, zs, x_ids, z_ids = peers_of(outer, inner)
    tp = lax.axis_index("tp")
    ts = [(tp + d) % tp_size for d in range(1, tp_size)]
    t_ids = [{"tp": v} for v in ts]

    loads = [
        pltpu.make_async_copy(wkv_ref, w_buf.at[:, pl.ds(0, 2 * cw)], w_sem.at[0]),
        pltpu.make_async_copy(wq_ref, w_buf.at[:, pl.ds(2 * cw, q_blocks * cw)], w_sem.at[1]),
    ]
    k_loads = [
        pltpu.make_async_copy(cache_ref.at[0, g], k_aug.at[g, :, pl.ds(0, dim)], k_sem.at[g])
        for g in range(kv_heads)
    ]
    v_loads = [
        pltpu.make_async_copy(cache_ref.at[1, g], v_raw.at[g], v_sem.at[g])
        for g in range(kv_heads)
    ]
    wo_load = pltpu.make_async_copy(wo_ref, wo_buf, wo_sem)
    for load in loads + k_loads + v_loads + [wo_load]:
        load.start()
    greet(x_ids + z_ids + t_ids)
    for load in loads:
        load.wait()

    def x1(b):
        return [remote(part_x.at[b, d], recv_x.at[b, d], (s1, r1), (b, d), p)
                for d, p in enumerate(x_ids)]

    def z1(b):
        return [remote(acc.at[b, zs[d]], recv_z.at[b, d], (s2, r2), (b, d), p)
                for d, p in enumerate(z_ids)]

    def zg(i):
        return [remote(q_buf.at[i, x, z], q_buf.at[i, x, z], (s3, r3), (i, d), p)
                for d, p in enumerate(z_ids)]

    def xg(i):
        return [remote(q_buf.at[i, x], q_buf.at[i, x], (s4, r4), (i, d), p)
                for d, p in enumerate(x_ids)]

    def xl(i):
        return [remote(lse.at[i, xs[d]], lse_recv.at[i, d], (s5, r5), (i, d), p)
                for d, p in enumerate(x_ids)]

    def xo(i):
        return [remote(o_buf.at[i, xs[d]], o_recv.at[i, d], (s6, r6), (i, d), p)
                for d, p in enumerate(x_ids)]

    def zl(i):
        return [remote(mid_lse.at[i], mid_lse_recv.at[i, d], (s7, r7), (i, d), p)
                for d, p in enumerate(z_ids)]

    def zo(i):
        return [remote(mid.at[i, zs[d]], mid_recv.at[i, d], (s8, r8), (i, d), p)
                for d, p in enumerate(z_ids)]

    def za(i):
        return [remote(att.at[x, i, z], att.at[x, i, z], (s9, r9), (i, d), p)
                for d, p in enumerate(z_ids)]

    def xa(i):
        return [remote(att.at[x, i], att.at[x, i], (sa, ra), (i, d), p)
                for d, p in enumerate(x_ids)]

    def start(copies):
        for copy in copies:
            copy.start()

    def arrive(copies):
        for copy in copies:
            copy.wait_recv()

    def ship(b):
        w = w_buf[:, pl.ds(pl.multiple_of(b * cw, cw), cw)]
        for d in range(inner - 1):
            part_x[b, d] = jnp.dot(hid_ref[xs[d]], w, preferred_element_type=jnp.float32)
        start(x1(b))
        own = jnp.dot(hid_ref[x], w, preferred_element_type=jnp.float32)
        acc[b] = own.reshape(outer, rows, cw)

    def add_x(b):
        arrive(x1(b))
        total = acc[b]
        for d in range(inner - 1):
            total += recv_x[b, d].reshape(outer, rows, cw)
        acc[b] = total
        start(z1(b))

    def add_z(b):
        arrive(z1(b))
        total = acc[b, z]
        for d in range(outer - 1):
            total += recv_z[b, d]
        low = total.astype(jnp.bfloat16)

        @pl.when(b < 2)
        def _():
            kv_new[b] = low

        @pl.when(b >= 2)
        def _():
            q_buf[b - 2, x, z] = low
            start(zg(b - 2))

    def spread(i):
        arrive(zg(i))
        start(xg(i))

    def attend(i):
        arrive(xg(i))
        g = i * per // group
        c = scale * LOG2E
        lane = lax.broadcasted_iota(jnp.int32, (tokens, dim), 1)
        one = jnp.where(lane == 0, 1.0, 0.0).astype(jnp.bfloat16)
        q = q_buf[i].reshape(tokens, cw)
        qs = [q[:, j * dim : (j + 1) * dim] for j in range(per)]
        aug = [jnp.concatenate([v, one], axis=1) for v in qs]
        k_fresh = kv_new[0, :, pl.ds(pl.multiple_of(g * dim, dim), dim)]
        v_fresh = kv_new[1, :, pl.ds(pl.multiple_of(g * dim, dim), dim)]
        v_fresh = v_fresh.astype(jnp.float32).T
        v_fresh = jnp.concatenate(
            [v_fresh, jnp.ones((16, rows), jnp.float32)], axis=0
        ).astype(jnp.bfloat16)
        seen = places[pl.ds((x * outer + z) * rows, rows), 0:1] <= posq_ref[...]

        def scores(j, b):
            if b < 0:
                return jnp.where(seen, lax.dot_general(
                    k_fresh, qs[j], NT, preferred_element_type=jnp.float32), HIDE)
            return lax.dot_general(
                k_aug[g, b * kb : (b + 1) * kb, :], aug[j], NT, preferred_element_type=jnp.float32
            )

        order = [(j, b) for b in list(range(slots // kb)) + [-1] for j in range(per)]
        state = [None] * per
        coming = scores(*order[0])
        for n, (j, b) in enumerate(order):
            s = coming
            if n + 1 < len(order):
                coming = scores(*order[n + 1])
            high = jnp.max(s, axis=0, keepdims=True)
            if state[j] is not None:
                high = jnp.maximum(state[j][0], high)
            p = jnp.exp2((s - high) * c).astype(jnp.bfloat16)
            v = v_fresh if b < 0 else v_aug[g, :, b * kb : (b + 1) * kb]
            t = jnp.dot(v, p, preferred_element_type=jnp.float32)
            if state[j] is not None:
                t = t + state[j][1] * jnp.exp2((state[j][0] - high) * c)
            state[j] = (high, t)
        for j in range(per):
            high, t = state[j]
            denom = t[dim : dim + 1, :]
            value = (t[:dim] / denom).astype(jnp.bfloat16)
            log = high * scale + jnp.log(denom)
            for v in range(inner):
                o_buf[i, v, j * dim : (j + 1) * dim, :] = value[:, v * half : (v + 1) * half]
                lse[i, v, j : j + 1, :] = log[:, v * half : (v + 1) * half]
        start(xl(i))
        start(xo(i))

    def shares(logs):
        top = functools.reduce(jnp.maximum, logs)
        parts = [jnp.exp(v - top) for v in logs]
        total = sum(parts[1:], parts[0])
        return [w / total for w in parts], top + jnp.log(total)

    def blend_x(i):
        arrive(xl(i))
        ws, log = shares([lse[i, x]] + [lse_recv[i, d] for d in range(inner - 1)])
        mid_lse[i] = log
        start(zl(i))
        arrive(xo(i))
        pieces = []
        for j in range(per):
            span = slice(j * dim, (j + 1) * dim)
            total = ws[0][j : j + 1] * o_buf[i, x, span, :].astype(jnp.float32)
            for d in range(inner - 1):
                total += ws[d + 1][j : j + 1] * o_recv[i, d, span, :].astype(jnp.float32)
            pieces.append(total.reshape(dim // chunk, chunk, half).astype(jnp.bfloat16))
        for j in range(per):
            n = dim // chunk
            mid[i, j * n : (j + 1) * n] = pieces[j]
        start(zo(i))

    def blend_z(i):
        arrive(zl(i))
        ws, _ = shares([mid_lse[i]] + [mid_lse_recv[i, d] for d in range(outer - 1)])
        for d in range(outer):
            weights[d] = ws[d]
        head = z * chunk // dim
        arrive(zo(i))
        total = weights[0, pl.ds(head, 1), :] * mid[i, z].astype(jnp.float32)
        for d in range(outer - 1):
            total += weights[d + 1, pl.ds(head, 1), :] * mid_recv[i, d].astype(jnp.float32)
        att[x, i, z] = total.astype(jnp.bfloat16)
        start(za(i))

    def spread_att(i):
        arrive(za(i))
        start(xa(i))

    def product(i, v):
        lhs = att[v, i].reshape(cw, half).T
        w = wo_buf[pl.ds(pl.multiple_of(i * cw, cw), cw), :]
        part[v] += jnp.dot(lhs, w, preferred_element_type=jnp.float32)

    def project_own(i):
        product(i, x)

    def project_rest(i):
        arrive(xa(i))
        for v in xs:
            product(i, v)

    ahead = 3
    for b in range(ahead):
        ship(b)
    lse[...] = jnp.zeros_like(lse)
    part[...] = jnp.zeros_like(part)
    places[...] = jnp.broadcast_to(posq_ref[...], (128, tokens)).T
    filled = filled_ref[0]
    row = lax.broadcasted_iota(jnp.int32, (slots, dim), 0)
    col = lax.broadcasted_iota(jnp.int32, (slots, dim), 1)
    bias = jnp.where((row >= filled) & (col == 0), HIDE, 0.0).astype(jnp.bfloat16)
    for g in range(kv_heads):
        k_aug[g, :, dim:] = bias
        v_aug[g, dim:, :] = jnp.ones((16, slots), jnp.bfloat16)
        v_loads[g].wait()
        v_aug[g, :dim, :] = v_raw[g].T
        k_loads[g].wait()
    wo_load.wait()

    def step(t, carry):
        def stage(lag, first, last, run):
            i = t - lag

            @pl.when((i >= first) & (i < last))
            def _():
                run(i)

        stage(-ahead, ahead, blocks, ship)
        stage(0, 0, blocks, add_x)
        stage(1, 0, blocks, add_z)
        stage(4, 0, q_blocks, spread)
        stage(5, 0, q_blocks, attend)
        stage(6, 0, q_blocks, blend_x)
        stage(7, 0, q_blocks, blend_z)
        stage(8, 0, q_blocks, spread_att)
        stage(8, 0, q_blocks, project_own)
        stage(9, 0, q_blocks, project_rest)
        return carry

    lax.fori_loop(0, q_blocks + 9, step, 0)

    share = out_ref.shape[0]
    whole = part[...].reshape(tp_size, share, part.shape[2])
    part_low[...] = whole.astype(jnp.bfloat16)
    last = [remote(part_low.at[ts[d]], recv_t.at[d], (st, rt), d, p) for d, p in enumerate(t_ids)]
    start(last)
    own = part.reshape(tp_size, share, part.shape[2])[tp]
    for d, copy in enumerate(last):
        copy.wait_recv()
        own += recv_t[d].astype(jnp.float32)
    out_ref[...] = own.astype(out_ref.dtype)
    for copy in last:
        copy.wait_send()

    def drain(kinds):
        def run(i, carry):
            for kind in kinds:
                for copy in kind(i):
                    copy.wait_send()
            return carry
        return run

    lax.fori_loop(0, blocks, drain([x1, z1]), 0)
    lax.fori_loop(0, q_blocks, drain([zg, xg, xl, xo, zl, zo, za, xa]), 0)


def body(hidden_input, w_query, key_value_weight, w_out, key_value_cache, filled, positions):
    tokens, width = hidden_input.shape
    shards = lax.axis_size("ctx")
    tp_size = lax.axis_size("tp")
    outer, inner = factor(shards)
    rows = tokens // shards
    half = outer * rows
    _, kv_heads, slots, dim = key_value_cache.shape
    cw = kv_heads * dim
    q_blocks = w_query.shape[1] // cw
    blocks = q_blocks + 2
    chunk = cw // outer
    out_width = w_out.shape[1]
    share = tokens // tp_size
    nx, nz, nt = max(inner - 1, 1), max(outer - 1, 1), max(tp_size - 1, 1)
    dma = pltpu.SemaphoreType.DMA
    vmem = pl.BlockSpec(memory_space=pltpu.VMEM)
    hbm = pl.BlockSpec(memory_space=pl.ANY)
    low, full = jnp.bfloat16, jnp.float32
    pairs = []
    for count, peers in (
        (blocks, nx), (blocks, nz), (q_blocks, nz), (q_blocks, nx), (q_blocks, nx),
        (q_blocks, nx), (q_blocks, nz), (q_blocks, nz), (q_blocks, nz), (q_blocks, nx),
    ):
        pairs += [dma((count, peers)), dma((count, peers))]
    return pl.pallas_call(
        functools.partial(
            layer_kernel, outer, inner, tp_size, kv_heads, dim, 1.0 / math.sqrt(dim),
            math.gcd(slots, 1024),
        ),
        out_shape=jax.ShapeDtypeStruct((share, out_width), low),
        in_specs=[pl.BlockSpec(memory_space=pltpu.SMEM), vmem, vmem, hbm, hbm, hbm, hbm],
        out_specs=vmem,
        scratch_shapes=[
            pltpu.VMEM((width, blocks * cw), low),
            pltpu.VMEM((kv_heads, slots, 2 * dim), low),
            pltpu.VMEM((kv_heads, slots, dim), low),
            pltpu.VMEM((kv_heads, dim + 16, slots), low),
            pltpu.VMEM(w_out.shape, low),
            pltpu.VMEM((blocks, nx, half, cw), full),
            pltpu.VMEM((blocks, nx, half, cw), full),
            pltpu.VMEM((blocks, outer, rows, cw), full),
            pltpu.VMEM((blocks, nz, rows, cw), full),
            pltpu.VMEM((2, rows, cw), low),
            pltpu.VMEM((q_blocks, inner, outer, rows, cw), low),
            pltpu.VMEM((q_blocks, inner, cw, half), low),
            pltpu.VMEM((q_blocks, inner, 8, half), full),
            pltpu.VMEM((q_blocks, nx, cw, half), low),
            pltpu.VMEM((q_blocks, nx, 8, half), full),
            pltpu.VMEM((q_blocks, outer, chunk, half), low),
            pltpu.VMEM((q_blocks, 8, half), full),
            pltpu.VMEM((q_blocks, nz, chunk, half), low),
            pltpu.VMEM((q_blocks, nz, 8, half), full),
            pltpu.VMEM((outer, 8, half), full),
            pltpu.VMEM((inner, q_blocks, outer, chunk, half), low),
            pltpu.VMEM((inner, half, out_width), full),
            pltpu.VMEM((tp_size, share, out_width), low),
            pltpu.VMEM((nt, share, out_width), low),
            pltpu.VMEM((tokens, 128), jnp.int32),
            dma((2,)), dma((kv_heads,)), dma((kv_heads,)), dma(()),
            *pairs,
            dma((nt,)), dma((nt,)),
        ],
        compiler_params=pltpu.CompilerParams(
            collective_id=0, has_side_effects=True, vmem_limit_bytes=60 << 20
        ),
        name="layer",
    )(
        filled, hidden_input.reshape(inner, half, width), positions.reshape(1, tokens),
        w_query, key_value_weight.reshape(width, -1),
        key_value_cache, w_out,
    )


def solution(mesh):
    placed = (
        P(None, "ctx"),
        P("ctx", "tp"),
        P("ctx", None, "tp"),
        P("tp", "ctx"),
        P(None, "tp", "ctx", None),
        P("ctx"),
        P(),
    )
    return jax.shard_map(
        body, mesh=mesh, in_specs=placed, out_specs=P("tp", "ctx"), check_vma=False
    )
```
